32 devices in a mesh: space: 8 (over y, x, core), tm: 4 (over z).
Axes of the slice: x: 2, y: 2, z: 4, core: 2. Of those that a mesh axis runs over, the one named last changes fastest.
Arguments:
- residual_in: float32 [32768, 2048], P('space', 'tm'), may hold values from -6 to 6
- factor_panel: float32 [32768, 1024], P('space'), may hold values from -0.1875 to 0.1875
- diag_inverse: float32 [4, 256, 256], replicated, may hold values from -2 to 2, as said below
- time_inverse: float32 [2048, 2048], P('space'), may hold values from -2 to 2, as said below
Outputs:
- whitened: float32 [32768, 2048], P(('space', 'tm'))
The draws below stay inside these ranges and needn't reach their ends.
Inputs may be any that keep to these rules, and one draw needn't show every extreme that they name: `diag_inverse`: lower triangular, with diagonal entries between 0.5 and 2. `time_inverse`: lower triangular, with diagonal entries between 0.5 and 2.
All inputs are finite; a program needn't handle non-finite values.
Results may differ from the reference program's by a relative error of at most 0.0001.
Values sent between devices are 32-bit elements; how exact they have to be, the bound alone decides.
No kernel may reach another device: no remote copies, remote signals or barrier semaphores. Data moves between devices by JAX's collectives and lax.ppermute only.
A program may use at most 128 MiB of HBM per device.

```python
import jax
import jax.numpy as jnp
from jax import lax

TIME = 2048
BS = 256
STEPS = 4
ROWS_DEV = 4096
ROWS = 32768
PANEL = 1024
N_SPACE = 8


def lower_factor(key, order, leading, reach):
    first, second = jax.random.split(key)
    shape = leading + (order, order)
    diagonal = jax.random.uniform(first, shape, jnp.float32, 0.8, 1.25)
    spread = reach * 3.0 ** 0.5 / order ** 0.5
    below = jax.random.uniform(second, shape, jnp.float32, -spread, spread)
    rowsix = jnp.arange(order, dtype=jnp.int32)[:, None]
    colsix = jnp.arange(order, dtype=jnp.int32)[None, :]
    return jnp.where(rowsix > colsix, below, 0.0) + jnp.where(rowsix == colsix, diagonal, 0.0)


def draw_diag_inverse(key, part):
    return lower_factor(jax.random.fold_in(key, 11), BS, (STEPS,), 0.5)


def draw_time_inverse(key, part):
    return lower_factor(jax.random.fold_in(key, 23), TIME, (), 0.7)


def steps_of(rng, shape, pieces, least, largest):
    gain, own = 1.0, jax.random.fold_in(rng, 6)
    for position, parts in pieces:
        steps = jnp.exp(jax.random.uniform(jax.random.fold_in(own, position), (parts,), jnp.float32, least / len(pieces), largest / len(pieces)))
        gain = gain * jnp.repeat(steps, shape[position] // parts).reshape([-1 if axis == position else 1 for axis in range(len(shape))])
    return gain


def noise(stream_key, dims, scale, bound, pieces=(), kind=jnp.bfloat16):
    values = scale * jax.random.normal(stream_key, dims, jnp.float32)
    if pieces:
        values = values * steps_of(stream_key, dims, pieces, -0.22, 0.18)
    return jnp.clip(values, -bound, bound).astype(kind)


def setup_inputs(seed: int = 0) -> dict:
    keys = jax.random.split(jax.random.key(seed), 5)
    return {
        "residual_in": noise(keys[0], (ROWS, TIME), 1.0, 6.0, ((0, 8), (1, 4)), jnp.float32),
        "factor_panel": noise(keys[1], (ROWS, PANEL), PANEL ** -0.5, 0.1875, ((0, 8),), jnp.float32),
        "diag_inverse": draw_diag_inverse(jax.random.fold_in(keys[4], 71), 0),
        "time_inverse": draw_time_inverse(jax.random.fold_in(keys[4], 71), 0),
    }


def reference(residual_in, factor_panel, diag_inverse, time_inverse):
    highest = lax.Precision.HIGHEST
    blocks = ROWS_DEV // BS
    shaped = residual_in.reshape(N_SPACE, blocks, BS, TIME)
    panel = factor_panel.reshape(N_SPACE, blocks, BS, PANEL)
    number = jnp.arange(blocks, dtype=jnp.int32)[None, :] * N_SPACE + jnp.arange(N_SPACE, dtype=jnp.int32)[:, None]
    number = number[:, :, None, None]
    for current in range(STEPS):
        solved = jnp.dot(diag_inverse[current], shaped[current, 0], precision=highest, preferred_element_type=jnp.float32)
        columns = panel[..., current * BS:(current + 1) * BS]
        update_term = jnp.einsum("sjab,bt->sjat", columns, solved, precision=highest)
        shaped = jnp.where(number > current, shaped - update_term, shaped)
        shaped = shaped.at[current, 0].set(solved)
    whitened_rows = shaped.reshape(ROWS, TIME)
    return jnp.dot(whitened_rows, time_inverse.T, precision=highest, preferred_element_type=jnp.float32)
```

```python
import functools

import jax
import jax.numpy as jnp
import numpy as np
from jax import lax
from jax.experimental import pallas as pl
from jax.experimental.pallas import tpu as pltpu
from jax.sharding import PartitionSpec as P


LANES = 128
CHUNKS = 4
F32 = jnp.float32
BF16 = jnp.bfloat16
NN = (((1,), (0,)), ((), ()))
NT = (((1,), (1,)), ((), ()))


def split(value):
    high = value.astype(BF16)
    low = (value - high.astype(F32)).astype(BF16)
    return high, low


def product(left, right, dims):
    def one(a, b):
        return lax.dot_general(a, b, dims, preferred_element_type=F32)

    return one(left[0], right[0]) + (one(left[0], right[1]) + one(left[1], right[0]))


def params(semantics=None):
    return pltpu.CompilerParams(dimension_semantics=semantics, vmem_limit_bytes=56 << 20)


def cost(flops, moved):
    return pl.CostEstimate(flops=int(flops), bytes_accessed=int(moved), transcendentals=0)


def solve(position, heads, tiles, diag_inverse):
    steps, width, _ = diag_inverse.shape
    columns = heads[0].shape[1]
    count = len(heads)

    def kernel(place, *refs):
        head_refs, tile_refs = refs[:count], refs[count : count + len(tiles) * count]
        diag, solved, high, low, rows, factor = refs[count + len(tiles) * count :]
        for away in range(count):
            block = lax.rem(place[0], count) ^ away
            rows[block] = head_refs[away][...]
            start = 0
            for part in range(len(tiles)):
                tile = tile_refs[part * count + away]
                factor[block, :, start : start + tile.shape[1]] = tile[...]
                start += tile.shape[1]
        for block in range(steps):
            value = rows[block]
            for before in range(block):
                left = split(factor[block, :, before * width : (before + 1) * width])
                span = pl.ds(before * width, width)
                value = value - product(left, (high[span, :], low[span, :]), NN)
            answer = product(split(diag[block]), split(value), NN)
            span = pl.ds(block * width, width)
            solved[span, :] = answer
            high[span, :], low[span, :] = split(answer)

    flat = [piece for tile in tiles for piece in tile]
    shape = (steps * width, columns)
    return pl.pallas_call(
        kernel,
        grid_spec=pltpu.PrefetchScalarGridSpec(
            num_scalar_prefetch=1,
            grid=(1,),
            in_specs=[pl.BlockSpec(x.shape, lambda i, p: (0, 0)) for x in [*heads, *flat]]
            + [pl.BlockSpec(diag_inverse.shape, lambda i, p: (0, 0, 0))],
            out_specs=[pl.BlockSpec(shape, lambda i, p: (0, 0))] * 3,
            scratch_shapes=[
                pltpu.VMEM((count, width, columns), F32),
                pltpu.VMEM((count, width, sum(t[0].shape[1] for t in tiles)), F32),
            ],
        ),
        out_shape=[jax.ShapeDtypeStruct(shape, x) for x in (F32, BF16, BF16)],
        compiler_params=params(),
        cost_estimate=cost(60 * width * width * columns, 16 * steps * width * columns),
        name="solve",
    )(position, *heads, *flat, diag_inverse)


def send_update(places, residual, factor, solved, high, low, chunk, size, raw, group, blocks):
    columns = residual.shape[1]
    depth = factor.shape[1]
    width = depth // blocks
    chunks = residual.shape[0] // group // size
    order = list(range(group - 1, 0, -1))
    first = [LANES if d in raw else 0 for d in order]

    def kernel(place, y, l, xf, xh, xl, *outs):
        left = split(l[...])
        for index, d in enumerate(order):

            @pl.when(pl.program_id(0) == index)
            def _():
                begin = first[index]
                right = (xh[:, begin:], xl[:, begin:])
                outs[index][...] = y[:, begin:] - product(left, right, NN)
                if chunk * size < width:

                    @pl.when(jnp.logical_and(place[1] == d, place[0] < blocks))
                    def _():
                        outs[index][...] = xf[:, begin:]

    def rows(i, p):
        return ((p[1] ^ (group - 1 - i)) * chunks + chunk, 0)

    def own(i, p):
        return (jnp.minimum(p[0], blocks - 1) * (width // size) + min(chunk, width // size - 1), 0)

    return pl.pallas_call(
        kernel,
        grid_spec=pltpu.PrefetchScalarGridSpec(
            num_scalar_prefetch=1,
            grid=(group - 1,),
            in_specs=[
                pl.BlockSpec((size, columns), rows),
                pl.BlockSpec((size, depth), rows),
                pl.BlockSpec((size, columns), own),
                pl.BlockSpec((depth, columns), lambda i, p: (0, 0)),
                pl.BlockSpec((depth, columns), lambda i, p: (0, 0)),
            ],
            out_specs=[pl.BlockSpec((size, columns - b), lambda i, p: (0, 0)) for b in first],
        ),
        out_shape=[jax.ShapeDtypeStruct((size, columns - b), F32) for b in first],
        compiler_params=params(("arbitrary",)),
        cost_estimate=cost(
            6 * (group - 1) * size * depth * columns,
            4 * (group - 1) * size * (2 * columns + depth) + 4 * depth * columns,
        ),
        name="send_update",
    )(places, residual, factor, solved, high, low)


def keep_update(places, pieces, sources, factor, solved, size, group, blocks):
    depth = factor.shape[1]
    width = depth // blocks
    keep = factor.shape[0] // group
    count = len(pieces)
    widths = [shape[1] for shape in sources]

    def kernel(place, *refs):
        ys, l, xs, x, outs, (xh, xl) = (
            refs[:count],
            refs[count],
            refs[count + 1],
            refs[count + 2],
            refs[count + 3 : 2 * count + 3],
            refs[2 * count + 3 :],
        )
        step = pl.program_id(0)

        @pl.when(step == 0)
        def _():
            xh[...], xl[...] = split(x[...])

        left = split(l[...])
        start = 0
        for y, out in zip(ys, outs):
            stop = start + out.shape[1]
            out[...] = y[...] - product(left, (xh[:, start:stop], xl[:, start:stop]), NN)

            @pl.when((place[1] == 0) & (place[0] < blocks) & (step < width // size))
            def _():
                out[...] = xs[:, start:stop]

            start = stop

    def mine(i, p):
        return (p[1] * (keep // size) + i, 0)

    def own(i, p):
        return (jnp.minimum(p[0], blocks - 1) * (width // size) + jnp.minimum(i, width // size - 1), 0)

    total = sum(widths)
    return pl.pallas_call(
        kernel,
        grid_spec=pltpu.PrefetchScalarGridSpec(
            num_scalar_prefetch=1,
            grid=(keep // size,),
            in_specs=[
                pl.BlockSpec((size, b), mine if shape[0] == factor.shape[0] else (lambda i, p: (i, 0)))
                for shape, b in zip(sources, widths)
            ]
            + [
                pl.BlockSpec((size, depth), mine),
                pl.BlockSpec((size, total), own),
                pl.BlockSpec((depth, total), lambda i, p: (0, 0)),
            ],
            out_specs=[pl.BlockSpec((size, b), lambda i, p: (i, 0)) for b in widths],
            scratch_shapes=[pltpu.VMEM((depth, total), BF16)] * 2,
        ),
        out_shape=[jax.ShapeDtypeStruct((keep, b), F32) for b in widths],
        compiler_params=params(("arbitrary",)),
        cost_estimate=cost(6 * keep * depth * total, 4 * keep * (2 * total + depth) + 4 * depth * total),
        name="keep_update",
    )(places, *pieces, factor, solved, solved)


def time_pieces(places, pieces, aways, held, order):
    rows = pieces[0].shape[0]
    count = len(pieces)

    def kernel(place, *refs):
        highs, lows = refs[-2], refs[-1]
        for index in range(count):

            @pl.when(pl.program_id(0) == index)
            def _():
                highs[...], lows[...] = split(refs[index][...])

    def where(i, p):
        return (p[2 + i], 0)

    index = jnp.concatenate([places, jnp.stack([places[0] ^ a for a in aways]).astype(jnp.int32)])
    shapes = [jax.ShapeDtypeStruct((order, order), BF16)] * 2
    aliases = {} if held is None else {1 + count: 0, 2 + count: 1}
    return pl.pallas_call(
        kernel,
        grid_spec=pltpu.PrefetchScalarGridSpec(
            num_scalar_prefetch=1,
            grid=(count,),
            in_specs=[pl.BlockSpec((rows, order), lambda i, p: (0, 0))] * count
            + [pl.BlockSpec(memory_space=pl.ANY)] * (0 if held is None else 2),
            out_specs=[pl.BlockSpec((rows, order), where)] * 2,
        ),
        out_shape=shapes,
        input_output_aliases=aliases,
        compiler_params=params(("arbitrary",)),
        cost_estimate=cost(4 * count * rows * order, 8 * count * rows * order),
        name="time_pieces",
    )(index, *pieces, *([] if held is None else held))


def finish(places, mine, lefts, rests, high, low, held, chunk, size, group, total_rows):
    order = high.shape[0]
    columns = order // group
    pairs = [(n, k) for n in range(group) for k in range(n + 1)]
    table = jnp.asarray(np.array([n for n, _ in pairs] + [k for _, k in pairs], np.int32))
    count = len(pairs)
    aways = sorted(rests)
    inputs, specs, layout = [mine], [pl.BlockSpec((size, columns), lambda i, p, q: (chunk, 0))], [(0, 0)]
    for d in aways:
        if d in lefts:
            inputs.append(lefts[d])
            specs.append(pl.BlockSpec((size, LANES), lambda i, p, q: (chunk, 0)))
            layout.append((d, 0))
        inputs.append(rests[d])
        specs.append(pl.BlockSpec(rests[d].shape, lambda i, p, q: (0, 0)))
        layout.append((d, columns - rests[d].shape[1]))
    loads = len(inputs)

    def kernel(place, pair, *refs):
        th, tl = refs[loads], refs[loads + 1]
        out, wh, wl = refs[-3:]
        step = pl.program_id(0)

        @pl.when(step == 0)
        def _():
            for ref, (d, start) in zip(refs[:loads], layout):
                span = slice(start, start + ref.shape[1])
                wh[place[1] ^ d, :, span], wl[place[1] ^ d, :, span] = split(ref[...])

        block = pair[count + step]
        value = product((wh[block], wl[block]), (th[...], tl[...]), NT)

        @pl.when(block == 0)
        def _():
            out[...] = value

        @pl.when(block > 0)
        def _():
            out[...] += value

    specs += [pl.BlockSpec((columns, columns), lambda i, p, q: (q[i], q[count + i]))] * 2
    aliases = {}
    extra = []
    if held is not None:
        specs.append(pl.BlockSpec(memory_space=pl.ANY))
        extra = [held]
        aliases = {2 + loads + 2: 0}
    return pl.pallas_call(
        kernel,
        grid_spec=pltpu.PrefetchScalarGridSpec(
            num_scalar_prefetch=2,
            grid=(count,),
            in_specs=specs,
            out_specs=pl.BlockSpec((size, columns), lambda i, p, q: (chunk, q[i])),
            scratch_shapes=[pltpu.VMEM((group, size, columns), BF16)] * 2,
        ),
        out_shape=jax.ShapeDtypeStruct((total_rows, order), F32),
        input_output_aliases=aliases,
        compiler_params=params(("arbitrary",)),
        cost_estimate=cost(6 * count * size * columns * columns, 8 * size * order + 4 * count * columns * columns),
        name="finish",
    )(places, table, *inputs, high, low, *extra)


def hop(value, axis, count, away, sources=None):
    keep = range(count) if sources is None else sources
    return lax.ppermute(value, axis, [(i, i ^ away) for i in keep])


def shards(spaces, group, residual_in, factor_panel, diag_inverse, time_inverse):
    blocks, width, _ = diag_inverse.shape
    rows, columns = residual_in.shape
    order = time_inverse.shape[1]
    keep = rows // group
    size = keep // CHUNKS
    here = lax.axis_index("space")
    slot = lax.axis_index("tm")
    places = jnp.stack([here, slot]).astype(jnp.int32)
    raw = [d for d in range(group - 1, 0, -1) if d >= group // 2]

    early = {}
    for d in raw:
        block = lax.dynamic_slice(residual_in, ((slot ^ d) * keep, 0), (keep, LANES))
        early[d] = hop(block, "tm", group, d)

    def spread(value, valid):
        held = value
        reach = blocks
        while reach < spaces:
            pairs = [(i, i + reach) for i in range(reach) if i % blocks in valid]
            moved = lax.ppermute(value if reach == blocks else held, "space", pairs)
            held = jnp.where(here >= reach, moved, held) if 2 * reach >= spaces else jnp.where(
                (here >= reach) & (here < 2 * reach), moved, held
            )
            reach *= 2
        got = {0: held}
        away = blocks // 2
        while away > 1:
            for known in list(got):
                near = hop(value if known == 0 else got[known], "space", spaces, away, [
                    i for i in range(blocks) if (i ^ known) in valid
                ])
                far_sources = [i for i in range(blocks, spaces) if ((i % blocks) ^ known) in valid]
                if far_sources:
                    far = hop(got[known], "space", spaces, away, far_sources)
                    near = jnp.where(here < blocks, near, far)
                got[known ^ away] = near
            away //= 2
        for known in list(got):
            got[known ^ 1] = hop(got[known], "space", spaces, 1)
        return [got[a] for a in range(blocks)]

    everyone = list(range(blocks))
    tile_rest = spread(factor_panel[:width, width : (blocks - 1) * width], everyone[2:])
    heads = spread(residual_in[:width], everyone)
    tile_first = spread(factor_panel[:width, :width], everyone[1:])
    solved, high, low = solve(places[:1], heads, [tile_first, tile_rest], diag_inverse)

    share = blocks * width // spaces
    mine = lax.dynamic_slice(solved, (here * share, 0), (share, LANES))
    crossed = jnp.concatenate([hop(mine, "tm", group, d) for d in raw], 1)

    rests = []
    for chunk in range(CHUNKS):
        outs = send_update(places, residual_in, factor_panel, solved, high, low, chunk, size, raw, group, blocks)
        rests.append({d: hop(out, "tm", group, d) for d, out in zip(range(group - 1, 0, -1), outs)})

    kept = keep_update(
        places, [residual_in], [residual_in.shape], factor_panel, solved, size, group, blocks
    )[0]

    pieces = {0: time_inverse}
    for d in range(2, spaces, 2):
        pieces[d] = hop(time_inverse, "space", spaces, d)
    held = None
    for d in range(0, spaces, 2):
        other = hop(pieces[d], "space", spaces, 1)
        held = time_pieces(places, [pieces[d], other], [d, d ^ 1], held, order)

    reach = 1
    while reach < spaces:
        other = hop(crossed, "space", spaces, reach)
        crossed = jnp.where(
            (here & reach) != 0,
            jnp.concatenate([other, crossed], 0),
            jnp.concatenate([crossed, other], 0),
        )
        reach *= 2
    lefts = dict(
        zip(
            raw,
            keep_update(
                places,
                [early[d] for d in raw],
                [early[d].shape for d in raw],
                factor_panel,
                crossed,
                size,
                group,
                blocks,
            ),
        )
    )

    out = None
    for chunk in range(CHUNKS):
        out = finish(places, kept, lefts, rests[chunk], *held, out, chunk, size, group, keep)
    return out


def solution(mesh):
    in_specs = (P("space", "tm"), P("space", None), P(), P("space", None))
    out_specs = P(("space", "tm"), None)
    body = functools.partial(shards, mesh.shape["space"], mesh.shape["tm"])
    return jax.shard_map(body, mesh=mesh, in_specs=in_specs, out_specs=out_specs, check_vma=False)
```
